32 devices in a mesh: gz: 8 (over z, x), gy: 4 (over y, core).
Axes of the slice: x: 2, y: 2, z: 4, core: 2. Of those that a mesh axis runs over, the one named last changes fastest.
Arguments:
- features: bfloat16 [128, 64, 32, 128], P('gz', 'gy'), may hold values from -6 to 6
- occupancy: int32 [8, 4, 4], P('gz', 'gy'), may hold values from 0 to 1, as said below
- kernel: bfloat16 [3, 3, 3, 64, 128], replicated, may hold values from -0.15625 to 0.15625
- upstream: bfloat16 [64, 32, 32, 128], P('gz', 'gy'), may hold values from -6 to 6
Outputs:
- coarse: bfloat16 [64, 32, 32, 128], P('gz', 'gy')
- feature_grad: bfloat16 [128, 64, 32, 128], P('gz', 'gy')
- kernel_grad: float32 [3, 3, 3, 64, 128], replicated
The draws below stay inside these ranges and needn't reach their ends.
Inputs may be any that keep to these rules, and one draw needn't show every extreme that they name: `occupancy`: each owner of 1 x 1 x 4 blocks holds at least one occupied block; owners' blocks are occupied at their own rates, so occupied counts differ between devices.
All inputs are finite; a program needn't handle non-finite values.
Results may differ from the reference program's by a relative error of at most 0.0022.
Values may be sent and summed in bfloat16 or wider, within the bound.
No kernel may reach another device: no remote copies, remote signals or barrier semaphores. Data moves between devices by JAX's collectives and lax.ppermute only.
A program may use at most 128 MiB of HBM per device.

```python
import jax
import jax.numpy as jnp
from jax import lax

C_IN = 64
C_OUT = 128
BE = 16
BZ = 1
BY = 1
BX = 4
NZ = 128
NY = 64
NX = 64


def draw_occupancy(key, part):
    owner_rows = NZ // BE // BZ
    owner_cols = NY // BE // BY
    rates = jax.random.randint(jax.random.fold_in(key, 11), (owner_rows, owner_cols, 1), 2, 9)
    rates = jnp.repeat(jnp.repeat(rates, BZ, axis=0), BY, axis=1)
    rolls = jax.random.randint(jax.random.fold_in(key, 12), (NZ // BE, NY // BE, BX), 0, 10)
    chosen = jax.random.randint(jax.random.fold_in(key, 13), (owner_rows, owner_cols, 1), 0, BX)
    chosen = jnp.repeat(jnp.repeat(chosen, BZ, axis=0), BY, axis=1)
    column = jnp.arange(BX, dtype=jnp.int32)[None, None, :]
    row_local = (jnp.arange(NZ // BE, dtype=jnp.int32) % BZ)[:, None, None]
    band_local = (jnp.arange(NY // BE, dtype=jnp.int32) % BY)[None, :, None]
    forced = (column == chosen) & (row_local == 0) & (band_local == 0)
    return ((rolls < rates) | forced).astype(jnp.int32)


def block_levels(key, extent, shards, low, high):
    factor_of = 1.0
    for dim, shards_of in shards:
        draws = jax.random.uniform(jax.random.fold_in(jax.random.fold_in(key, 6), dim), (shards_of,), jnp.float32, low / len(shards), high / len(shards))
        factor_of = factor_of * jnp.repeat(jnp.exp(draws), extent[dim] // shards_of).reshape((-1,) + (1,) * (len(extent) - 1 - dim))
    return factor_of


def centred(stream_key, dims, spread, reach, shards=(), kind=jnp.bfloat16):
    loudness = block_levels(stream_key, dims, shards, -0.22, 0.18) if shards else 1.0
    values = jax.random.normal(stream_key, dims, jnp.float32) * spread * loudness
    return jnp.minimum(jnp.maximum(values, -reach), reach).astype(kind)


def setup_inputs(seed: int = 0) -> dict:
    arg_keys = jax.random.split(jax.random.key(seed), 5)
    return {
        "features": centred(arg_keys[0], (NZ, NY, NX // 2, 2 * C_IN), 1.0, 6.0, ((0, 8), (1, 4))),
        "occupancy": draw_occupancy(jax.random.fold_in(arg_keys[4], 71), 0),
        "kernel": centred(arg_keys[2], (3, 3, 3, C_IN, C_OUT), (27 * C_IN) ** -0.5, 0.15625),
        "upstream": centred(arg_keys[3], (NZ // 2, NY // 2, NX // 2, C_OUT), 1.0, 6.0, ((0, 8), (1, 4))),
    }


def expand(mask, edge, xedge):
    full = jnp.repeat(mask, edge, axis=0)
    full = jnp.repeat(full, edge, axis=1)
    return jnp.repeat(full, xedge, axis=2)

def strided(ext, kz, ky, zo, yo):
    return lax.slice(ext, (kz, ky, 0, 0), (kz + 2 * zo - 1, ky + 2 * yo - 1, ext.shape[2], ext.shape[3]), (2, 2, 1, 1))

def shifted_odd(piece, cin):
    odd = piece[..., cin:]
    return jnp.concatenate([jnp.zeros_like(odd[:, :, :1]), odd[:, :, :-1]], 2)

def convolve(ext, kernel):
    zo = (ext.shape[0] - 1) // 2
    yo = (ext.shape[1] - 1) // 2
    pairs = ext.shape[2]
    cin = kernel.shape[3]
    cout = kernel.shape[4]
    total = jnp.zeros((zo * yo * pairs, cout), jnp.float32)
    for kz in range(3):
        for ky in range(3):
            piece = strided(ext, kz, ky, zo, yo)
            pair_w = jnp.concatenate([kernel[kz, ky, 1], kernel[kz, ky, 2]], 0)
            total = total + jnp.dot(piece.reshape(-1, 2 * cin), pair_w, preferred_element_type=jnp.float32)
            total = total + jnp.dot(shifted_odd(piece, cin).reshape(-1, cin), kernel[kz, ky, 0], preferred_element_type=jnp.float32)
    return total.reshape(zo, yo, pairs, cout)

def data_grad(kernel, grad):
    zo, yo, pairs, cout = grad.shape
    cin = kernel.shape[3]
    flat = grad.reshape(-1, cout)
    dext = jnp.zeros((2 * zo + 1, 2 * yo + 1, pairs, 2 * cin), jnp.float32)
    for kz in range(3):
        for ky in range(3):
            pair_w = jnp.concatenate([kernel[kz, ky, 1], kernel[kz, ky, 2]], 0)
            d_pair = jnp.dot(flat, pair_w.T, preferred_element_type=jnp.float32).reshape(zo, yo, pairs, 2 * cin)
            d_odd = jnp.dot(flat, kernel[kz, ky, 0].T, preferred_element_type=jnp.float32).reshape(zo, yo, pairs, cin)
            back = jnp.concatenate([d_odd[:, :, 1:], jnp.zeros_like(d_odd[:, :, :1])], 2)
            piece = d_pair + jnp.concatenate([jnp.zeros_like(back), back], 3)
            placed = lax.pad(piece, jnp.float32(0.0), ((kz, 2 - kz, 1), (ky, 2 - ky, 1), (0, 0, 0), (0, 0, 0)))
            dext = dext + placed
    return dext

def weight_grad(ext, grad, cin):
    zo, yo, pairs, cout = grad.shape
    flat = grad.reshape(-1, cout)
    parts_list = []
    for kz in range(3):
        for ky in range(3):
            piece = strided(ext, kz, ky, zo, yo)
            d_pair = jnp.dot(piece.reshape(-1, 2 * cin).T, flat, preferred_element_type=jnp.float32)
            d_odd = jnp.dot(shifted_odd(piece, cin).reshape(-1, cin).T, flat, preferred_element_type=jnp.float32)
            parts_list.append(jnp.stack([d_odd, d_pair[:cin], d_pair[cin:]], 0))
    return jnp.stack(parts_list, 0).reshape(3, 3, 3, cin, cout)

def reference(features, occupancy, kernel, upstream):
    cin = kernel.shape[3]
    in_mask = expand(occupancy, BE, BE // 2).astype(jnp.bfloat16)[..., None]
    out_mask = expand(occupancy, BE // 2, BE // 2).astype(jnp.bfloat16)[..., None]
    active = features * in_mask
    ext = jnp.pad(active, ((1, 0), (1, 0), (0, 0), (0, 0)))
    coarse = (convolve(ext, kernel) * out_mask.astype(jnp.float32)).astype(jnp.bfloat16)
    grad = upstream * out_mask
    dext = data_grad(kernel, grad)
    feature_grad = (dext[1:, 1:] * in_mask.astype(jnp.float32)).astype(jnp.bfloat16)
    kernel_grad = weight_grad(ext, grad, cin)
    return (coarse, feature_grad, kernel_grad)
```

```python
import functools

import jax
import jax.numpy as jnp
from jax import lax
from jax.experimental import pallas as pl
from jax.experimental.pallas import tpu as pltpu
from jax.sharding import PartitionSpec as P

F32 = jnp.float32
BF16 = jnp.bfloat16

TAPS = ((1, 1), (1, 2), (2, 1), (2, 2), (1, 0), (2, 0), (0, 1), (0, 2), (0, 0))


def row_mask(occ_ref, pairs, lanes):
    width = pairs // occ_ref.shape[2]
    block = lax.broadcasted_iota(jnp.int32, (pairs, lanes), 0) // width
    mask = jnp.zeros((pairs, lanes), F32)
    for k in range(occ_ref.shape[2]):
        here = occ_ref[0, 0, k].astype(F32)
        mask = jnp.where(block == k, here, mask)
    return mask


def with_next(g):
    pairs = g.shape[-2]
    axis = g.ndim - 2
    wide = pltpu.roll(g.astype(F32), pairs - 1, axis)
    last = lax.broadcasted_iota(jnp.int32, wide.shape, axis) == pairs - 1
    return jnp.concatenate([g, jnp.where(last, 0.0, wide).astype(BF16)], -1)


def fill_grads(gext, g_ref, gz_ref, gy_ref, occ_ref):
    zo, yo, pairs, cout = g_ref.shape
    mask = row_mask(occ_ref, pairs, cout).astype(BF16)
    for a in range(zo):
        gext[a, :yo] = with_next(g_ref[a] * mask)
    gext[zo, :yo] = with_next(gz_ref[...])
    gext[:, yo] = with_next(gy_ref[...])


def grad_rows(gext, a0, na, da, db):
    _, yo1, pairs, wide = gext.shape
    yo = yo1 - 1
    return gext[pl.ds(a0 + da, na), db : db + yo].reshape(na * yo * pairs, wide)


def fill_taps(taps, k_ref):
    cin, cout = k_ref.shape[1:]
    for s, (kz, ky) in enumerate(TAPS):
        t = 3 * (3 * kz + ky)
        r = s * 2 * cin
        taps[r : r + 2 * cin, :cout] = k_ref[t + 1 : t + 3].reshape(2 * cin, cout)
        taps[r : r + cin, cout:] = jnp.zeros((cin, cout), BF16)
        taps[r + cin : r + 2 * cin, cout:] = k_ref[t]


def weight_kernel(occ_ref, f_ref, g_ref, gz_ref, gy_ref, keep_ref, send_ref, gext, acc, flat):
    step = pl.program_id(0)
    na, _, yo, _, pairs, chans = f_ref.shape
    cin = chans // 2
    cout = g_ref.shape[3]

    @pl.when(step == 0)
    def _():
        fill_grads(gext, g_ref, gz_ref, gy_ref, occ_ref)
        acc[...] = jnp.zeros_like(acc)

    mask = row_mask(occ_ref, pairs, chans).astype(BF16)

    def rows(pz, py):
        return (f_ref[:, pz, :, py] * mask).reshape(na * yo * pairs, chans)

    ee, eo, oe, oo = rows(0, 0), rows(0, 1), rows(1, 0), rows(1, 1)
    a0 = step * na

    def product(x, da, db):
        g = grad_rows(gext, a0, na, da, db)
        return lax.dot_general(x, g, (((0,), (0,)), ((), ())), preferred_element_type=F32)

    c = chans
    acc[: 4 * c] += product(jnp.concatenate([ee, eo, oe, oo], 1), 0, 0)
    acc[4 * c : 6 * c] += product(jnp.concatenate([eo, oo], 1), 0, 1)
    acc[6 * c : 8 * c] += product(jnp.concatenate([oe, oo], 1), 1, 0)
    acc[8 * c : 9 * c] += product(oo, 1, 1)

    @pl.when(step == pl.num_programs(0) - 1)
    def _():
        for s, (kz, ky) in enumerate(TAPS):
            t = 3 * (3 * kz + ky) * cin
            r = s * chans
            flat[t : t + cin] = acc[r + cin : r + chans, cout:]
            flat[t + cin : t + 3 * cin] = acc[r : r + chans, :cout]
        half = keep_ref.shape[0]
        bit = lax.axis_index("gy") % 2
        keep_ref[...] = flat[pl.ds(pl.multiple_of(bit * half, 8), half)]
        send_ref[...] = flat[pl.ds(pl.multiple_of((1 - bit) * half, 8), half)]


def data_kernel(occ_ref, k_ref, g_ref, gz_ref, gy_ref, out_ref, gext, taps):
    step = pl.program_id(0)
    na, _, yo, _, pairs, chans = out_ref.shape

    @pl.when(step == 0)
    def _():
        fill_grads(gext, g_ref, gz_ref, gy_ref, occ_ref)
        fill_taps(taps, k_ref)

    a0 = step * na
    c = chans

    def product(da, db, first, count):
        g = grad_rows(gext, a0, na, da, db)
        w = taps[first * c : (first + count) * c]
        return lax.dot_general(g, w, (((1,), (1,)), ((), ())), preferred_element_type=F32)

    mask = row_mask(occ_ref, pairs, chans)
    p00 = product(0, 0, 0, 4)
    p01 = product(0, 1, 4, 2)
    p10 = product(1, 0, 6, 2)
    p11 = product(1, 1, 8, 1)

    def put(pz, py, value):
        out_ref[:, pz, :, py] = (value.reshape(na, yo, pairs, chans) * mask).astype(BF16)

    put(0, 0, p00[:, :c])
    put(0, 1, p00[:, c : 2 * c] + p01[:, :c])
    put(1, 0, p00[:, 2 * c : 3 * c] + p10[:, :c])
    put(1, 1, (p00[:, 3 * c :] + p01[:, c:]) + (p10[:, c:] + p11))


def coarse_kernel(occ_ref, k_ref, f_ref, fz_ref, fy_ref, out_ref, prev, taps):
    step = pl.program_id(0)
    na, _, yo, _, pairs, chans = f_ref.shape
    cout = out_ref.shape[3]

    @pl.when(step == 0)
    def _():
        fill_taps(taps, k_ref)
        prev[...] = fz_ref[...]

    mask = row_mask(occ_ref, pairs, chans).astype(BF16)
    even = f_ref[:, 0] * mask
    odd = f_ref[:, 1] * mask
    before = prev[...][None]
    if na > 1:
        before = jnp.concatenate([before, odd[:-1]], 0)
    prev[...] = odd[na - 1]
    z0 = 2 * na * step
    fy = fy_ref[pl.ds(z0, 2 * na + 1)]

    def rows(planes, rim, ky):
        if ky == 1:
            x = planes[:, :, 0]
        elif ky == 2:
            x = planes[:, :, 1]
        else:
            x = jnp.concatenate([rim[:, None], planes[:, :-1, 1]], 1)
        return x.reshape(na * yo * pairs, chans)

    rims = fy[1:].reshape(na, 2, pairs, chans)
    edge = fy[: 2 * na].reshape(na, 2, pairs, chans)
    planes = {0: (before, edge[:, 0]), 1: (even, rims[:, 0]), 2: (odd, rims[:, 1])}
    lhs = jnp.concatenate([rows(*planes[kz], ky) for kz, ky in TAPS], 1)
    both = jnp.dot(lhs, taps[...], preferred_element_type=F32)
    both = both.reshape(na * yo, pairs, 2 * cout)
    later = pltpu.roll(both[..., cout:], 1, 1)
    first = lax.broadcasted_iota(jnp.int32, later.shape, 1) == 0
    total = both[..., :cout] + jnp.where(first, 0.0, later)
    out = total * row_mask(occ_ref, pairs, cout)
    out_ref[...] = out.reshape(na, yo, pairs, cout).astype(BF16)


def whole(shape):
    return pl.BlockSpec(shape, lambda i: (0,) * len(shape))


def leading(shape, n):
    block = (n,) + tuple(shape[1:])
    return pl.BlockSpec(block, lambda i: (i,) + (0,) * (len(shape) - 1))


SCALARS = pl.BlockSpec(memory_space=pltpu.SMEM)
PARAMS = pltpu.CompilerParams(dimension_semantics=("arbitrary",), vmem_limit_bytes=40 << 20)


def cost(flops, nbytes):
    return pl.CostEstimate(flops=int(flops), bytes_accessed=int(nbytes), transcendentals=0)


def weight_grad(occ, split, grad, gz, gy, cin, na=2):
    zo, yo, pairs, cout = grad.shape
    chans = 2 * cin
    half = 27 * cin // 2
    part = jax.ShapeDtypeStruct((half, cout), F32)
    return pl.pallas_call(
        weight_kernel,
        grid=(zo // na,),
        in_specs=[SCALARS, leading(split.shape, na), whole(grad.shape), whole(gz.shape), whole(gy.shape)],
        out_specs=[whole(part.shape)] * 2,
        out_shape=[part, part],
        scratch_shapes=[
            pltpu.VMEM((zo + 1, yo + 1, pairs, 2 * cout), BF16),
            pltpu.VMEM((9 * chans, 2 * cout), F32),
            pltpu.VMEM((2 * half, cout), F32),
        ],
        compiler_params=PARAMS,
        cost_estimate=cost(2 * zo * yo * pairs * 9 * chans * 2 * cout, 2 * split.size),
    )(occ, split, grad, gz, gy)


def data_grad(occ, kernel, grad, gz, gy, na=1):
    zo, yo, pairs, cout = grad.shape
    cin = kernel.shape[1]
    chans = 2 * cin
    shape = (zo, 2, yo, 2, pairs, chans)
    return pl.pallas_call(
        data_kernel,
        grid=(zo // na,),
        in_specs=[SCALARS, whole(kernel.shape), whole(grad.shape), whole(gz.shape), whole(gy.shape)],
        out_specs=leading(shape, na),
        out_shape=jax.ShapeDtypeStruct(shape, BF16),
        scratch_shapes=[
            pltpu.VMEM((zo + 1, yo + 1, pairs, 2 * cout), BF16),
            pltpu.VMEM((9 * chans, 2 * cout), BF16),
        ],
        compiler_params=PARAMS,
        cost_estimate=cost(2 * zo * yo * pairs * 9 * chans * 2 * cout, 2 * zo * yo * pairs * 4 * chans),
    )(occ, kernel, grad, gz, gy)


def coarse_conv(occ, kernel, split, fz, fy, na=2):
    zo, _, yo, _, pairs, chans = split.shape
    cout = kernel.shape[2]
    shape = (zo, yo, pairs, cout)
    return pl.pallas_call(
        coarse_kernel,
        grid=(zo // na,),
        in_specs=[SCALARS, whole(kernel.shape), leading(split.shape, na), whole(fz.shape), whole(fy.shape)],
        out_specs=leading(shape, na),
        out_shape=jax.ShapeDtypeStruct(shape, BF16),
        scratch_shapes=[
            pltpu.VMEM((yo, 2, pairs, chans), BF16),
            pltpu.VMEM((9 * chans, 2 * cout), BF16),
        ],
        compiler_params=PARAMS,
        cost_estimate=cost(2 * zo * yo * pairs * 9 * chans * 2 * cout, 2 * split.size),
    )(occ, kernel, split, fz, fy)


def shifted(block, axis, distance):
    n = lax.axis_size(axis)
    return lax.ppermute(block, axis, [(i, i + distance) for i in range(n) if 0 <= i + distance < n])


def partners(nz, ny, other):
    moves = []
    for z in range(nz):
        for y in range(ny):
            pz, py = other(z, y)
            moves.append((z * ny + y, pz * ny + py))
    return moves


def join_kernel(a_ref, b_ref, c_ref, d_ref, out_ref, *, nz, ny):
    z, y = lax.axis_index("gz"), lax.axis_index("gy")
    core = y % 2
    up, along = (y // 2) % 2, z % 2
    first = jnp.where(core == 0, along, up)
    second = jnp.where(core == 0, up, along)
    part = a_ref.shape[0]

    def put(c, f, s, value):
        at = pl.multiple_of(((c * 2 + f) * 2 + s) * part, 8)
        out_ref[pl.ds(at, part)] = value.astype(F32)

    put(core, first, second, a_ref[...])
    put(core, first, 1 - second, b_ref[...])
    put(core, 1 - first, second, c_ref[:part])
    put(core, 1 - first, 1 - second, c_ref[part:])
    put(1 - core, second, first, d_ref[:part])
    put(1 - core, second, 1 - first, d_ref[part : 2 * part])
    put(1 - core, 1 - second, first, d_ref[2 * part : 3 * part])
    put(1 - core, 1 - second, 1 - first, d_ref[3 * part :])


def summed(keep, send):
    both = ("gz", "gy")
    nz, ny = lax.axis_size("gz"), lax.axis_size("gy")
    z, y = lax.axis_index("gz"), lax.axis_index("gy")
    core, up, along = y % 2, (y // 2) % 2, z % 2
    first = jnp.where(core == 0, along, up)
    second = jnp.where(core == 0, up, along)

    to_core = partners(nz, ny, lambda z, y: (z, y ^ 1))
    to_first = partners(nz, ny, lambda z, y: (z ^ 1, y) if y % 2 == 0 else (z, y ^ 2))
    to_second = partners(nz, ny, lambda z, y: (z, y ^ 2) if y % 2 == 0 else (z ^ 1, y))

    def half(x, bit):
        n = x.shape[0] // 2
        return lax.dynamic_slice_in_dim(x, bit * n, n, 0)

    got = lax.ppermute(send, both, to_core)
    for route, bit in ((to_first, first), (to_second, second)):
        send = half(keep, 1 - bit) + half(got, 1 - bit)
        keep = half(keep, bit) + half(got, bit)
        got = lax.ppermute(send, both, route)
    total = keep + got
    step = 2
    while step < nz:
        total = total + lax.ppermute(total, both, partners(nz, ny, lambda z, y: (z ^ step, y)))
        step *= 2

    a = total.astype(BF16)
    b = lax.ppermute(a, both, to_second)
    ab = jnp.concatenate([a, b], 0)
    c = lax.ppermute(ab, both, to_first)
    d = lax.ppermute(jnp.concatenate([ab, c], 0), both, to_core)
    vmem = pl.BlockSpec(memory_space=pltpu.VMEM)
    return pl.pallas_call(
        functools.partial(join_kernel, nz=nz, ny=ny),
        in_specs=[vmem] * 4,
        out_specs=vmem,
        out_shape=jax.ShapeDtypeStruct((8 * a.shape[0], a.shape[1]), F32),
        compiler_params=pltpu.CompilerParams(vmem_limit_bytes=16 << 20),
        cost_estimate=cost(0, 8 * a.size * 6),
    )(a, b, c, d)


def shards(features, occupancy, kernel, upstream):
    nz, ny = lax.axis_size("gz"), lax.axis_size("gy")
    if ny != 4 or nz & (nz - 1) or occupancy.shape[:2] != (1, 1):
        raise ValueError("unsupported mesh")
    zi, yi, pairs, chans = features.shape
    zo, yo = zi // 2, yi // 2
    taps = kernel.reshape((27,) + kernel.shape[3:])
    split = features.reshape(zo, 2, yo, 2, pairs, chans)
    mask = jnp.repeat(occupancy[0, 0], pairs // occupancy.shape[2]).astype(BF16)[None, :, None]

    gz = shifted(upstream[0] * mask, "gz", -1)
    gy = shifted(jnp.concatenate([upstream[:, 0] * mask, gz[:1]], 0), "gy", -1)
    keep, send = weight_grad(occupancy, split, upstream, gz, gy, chans // 2)
    kernel_grad = summed(keep, send).reshape(kernel.shape)

    fz = shifted(features[-1] * mask, "gz", 1)
    fy = shifted(jnp.concatenate([fz[-1:], features[:, -1] * mask], 0), "gy", 1)
    coarse = coarse_conv(occupancy, taps, split, fz.reshape(yo, 2, pairs, chans), fy)
    feature_grad = data_grad(occupancy, taps, upstream, gz, gy).reshape(features.shape)
    return (coarse, feature_grad, kernel_grad)


def solution(mesh):
    return jax.shard_map(
        shards,
        mesh=mesh,
        in_specs=(P("gz", "gy", None, None), P("gz", "gy", None), P(), P("gz", "gy", None, None)),
        out_specs=(P("gz", "gy", None, None), P("gz", "gy", None, None), P()),
        check_vma=False,
    )
```

```python
import jax
import jax.numpy as jnp
from jax import lax
from jax.experimental import pallas as pl
from jax.experimental.pallas import tpu as pltpu
from jax.sharding import PartitionSpec as P


F32 = jnp.float32
BF16 = jnp.bfloat16

TAPS = ((1, 1), (1, 2), (2, 1), (2, 2), (1, 0), (2, 0), (0, 1), (0, 2), (0, 0))


def row_mask(occ_ref, pairs, lanes):
    width = pairs // occ_ref.shape[2]
    block = lax.broadcasted_iota(jnp.int32, (pairs, lanes), 0) // width
    mask = jnp.zeros((pairs, lanes), F32)
    for k in range(occ_ref.shape[2]):
        here = occ_ref[0, 0, k].astype(F32)
        mask = jnp.where(block == k, here, mask)
    return mask


def with_next(g):
    pairs = g.shape[-2]
    axis = g.ndim - 2
    wide = pltpu.roll(g.astype(F32), pairs - 1, axis)
    last = lax.broadcasted_iota(jnp.int32, wide.shape, axis) == pairs - 1
    return jnp.concatenate([g, jnp.where(last, 0.0, wide).astype(BF16)], -1)


def fill_grads(gext, g_ref, gz_ref, gy_ref, occ_ref):
    zo, yo, pairs, cout = g_ref.shape
    mask = row_mask(occ_ref, pairs, cout).astype(BF16)
    for a in range(zo):
        gext[a, :yo] = with_next(g_ref[a] * mask)
    gext[:zo, yo] = with_next(gy_ref[...])
    gext[zo] = with_next(gz_ref[...])


def grad_rows(gext, a0, na, da, db):
    _, yo1, pairs, wide = gext.shape
    yo = yo1 - 1
    return gext[pl.ds(a0 + da, na), db : db + yo].reshape(na * yo * pairs, wide)


def fill_taps(taps, k_ref):
    cin, cout = k_ref.shape[1:]
    for s, (kz, ky) in enumerate(TAPS):
        t = 3 * (3 * kz + ky)
        r = s * 2 * cin
        taps[r : r + 2 * cin, :cout] = k_ref[t + 1 : t + 3].reshape(2 * cin, cout)
        taps[r : r + cin, cout:] = jnp.zeros((cin, cout), BF16)
        taps[r + cin : r + 2 * cin, cout:] = k_ref[t]


def rims_of(occ, features, grad):
    zi, yi, pairs, chans = features.shape
    zo, yo, _, cout = grad.shape
    sizes = ((yo, pairs, cout), (zo, pairs, cout), (yi, pairs, chans), (zi, pairs, chans))

    def body(occ_ref, fl_ref, fb_ref, ga_ref, gb_ref, gz_ref, gy_ref, fz_ref, fy_ref):
        mask = row_mask(occ_ref, pairs, chans).astype(BF16)
        gz_ref[...] = ga_ref[0] * mask
        gy_ref[...] = gb_ref[:, 0] * mask
        fz_ref[...] = fl_ref[0] * mask
        fy_ref[...] = fb_ref[:, 0] * mask

    return pl.pallas_call(
        body,
        grid=(1,),
        in_specs=[
            SCALARS,
            pl.BlockSpec((1, yi, pairs, chans), lambda i: (zi - 1, 0, 0, 0)),
            pl.BlockSpec((zi, 1, pairs, chans), lambda i: (0, yi - 1, 0, 0)),
            pl.BlockSpec((1, yo, pairs, cout), lambda i: (0, 0, 0, 0)),
            pl.BlockSpec((zo, 1, pairs, cout), lambda i: (0, 0, 0, 0)),
        ],
        out_specs=[whole(x) for x in sizes],
        out_shape=[jax.ShapeDtypeStruct(x, BF16) for x in sizes],
        compiler_params=pltpu.CompilerParams(vmem_limit_bytes=4 << 20),
        cost_estimate=cost(0, 2 * 2 * sum(x[0] * x[1] * x[2] for x in sizes)),
    )(in_hbm(occ), in_hbm(features), in_hbm(features), in_hbm(grad), in_hbm(grad))


def weight_kernel(occ_ref, f_ref, g_ref, acc_ref, gext):
    step = pl.program_id(0)
    na, _, yo, _, pairs, chans = f_ref.shape
    zo, _, _, cout = g_ref.shape

    @pl.when(step == 0)
    def _():
        mask = row_mask(occ_ref, pairs, cout).astype(BF16)
        for a in range(zo):
            gext[a, :yo] = with_next(g_ref[a] * mask)
        gext[zo] = jnp.zeros(gext.shape[1:], BF16)
        gext[:, yo] = jnp.zeros((zo + 1, pairs, 2 * cout), BF16)
        acc_ref[...] = jnp.zeros_like(acc_ref)

    mask = row_mask(occ_ref, pairs, chans).astype(BF16)

    def rows(pz, py):
        return (f_ref[:, pz, :, py] * mask).reshape(na * yo * pairs, chans)

    ee, eo, oe, oo = rows(0, 0), rows(0, 1), rows(1, 0), rows(1, 1)
    a0 = step * na
    c = chans

    def product(x, da, db):
        return rows_product(x, grad_rows(gext, a0, na, da, db))

    acc_ref[: 4 * c] += product(jnp.concatenate([ee, eo, oe, oo], 1), 0, 0)
    acc_ref[4 * c : 6 * c] += product(jnp.concatenate([eo, oo], 1), 0, 1)
    acc_ref[6 * c : 8 * c] += product(jnp.concatenate([oe, oo], 1), 1, 0)
    acc_ref[8 * c : 9 * c] += product(oo, 1, 1)


def rows_product(x, g):
    return lax.dot_general(x, g, (((0,), (0,)), ((), ())), preferred_element_type=F32)


def place():
    z, y = lax.axis_index("gz"), lax.axis_index("gy")
    core, up, along = y % 2, (y // 2) % 2, z % 2
    first = jnp.where(core == 0, along, up)
    second = jnp.where(core == 0, up, along)
    return core, first, second


def edge_kernel(acc_ref, fz_ref, fy_ref, gz_ref, gy_ref, keep_ref, send_ref, acc, flat):
    yi, pairs, chans = fz_ref.shape
    cin, cout, yo, zo = chans // 2, gz_ref.shape[2], yi // 2, gy_ref.shape[0]
    c = chans
    fz = fz_ref[...].reshape(yo, 2, pairs, chans)
    fy = fy_ref[...].reshape(zo, 2, pairs, chans)
    gz, gy = with_next(gz_ref[...]), with_next(gy_ref[...])

    def flatten(x):
        return x.reshape(x.shape[0] * pairs, x.shape[-1])

    oe, oo = flatten(fz[:, 0]), flatten(fz[:, 1])
    acc[6 * c : 8 * c] = acc_ref[6 * c : 8 * c] + rows_product(jnp.concatenate([oe, oo], 1), flatten(gz[:yo]))
    last = rows_product(oo, flatten(gz[1:]))
    eo, oo = flatten(fy[:, 0]), flatten(fy[:, 1])
    acc[4 * c : 6 * c] = acc_ref[4 * c : 6 * c] + rows_product(jnp.concatenate([eo, oo], 1), flatten(gy))
    last = last + rows_product(oo[: -pairs], flatten(gy[1:]))
    acc[8 * c :] = acc_ref[8 * c :] + last

    for s, (kz, ky) in enumerate(TAPS):
        t = 3 * (3 * kz + ky) * cin
        r = s * chans
        source = acc_ref if s < 4 else acc
        flat[t : t + cin] = source[r + cin : r + chans, cout:]
        flat[t + cin : t + 3 * cin] = source[r : r + chans, :cout]
    core, first, second = place()
    part = keep_ref.shape[0] // 4
    for f in range(2):
        for s in range(2):
            to = (2 * f + s) * part
            mine = ((core * 2 + (first ^ f)) * 2 + (second ^ s)) * part
            keep_ref[to : to + part] = flat[pl.ds(pl.multiple_of(mine, 8), part)]
            its = (((1 - core) * 2 + (second ^ f)) * 2 + (first ^ s)) * part
            send_ref[to : to + part] = flat[pl.ds(pl.multiple_of(its, 8), part)]


def data_kernel(occ_ref, k_ref, g_ref, gz_ref, gy_ref, out_ref, gext, taps):
    step = pl.program_id(0)
    na, _, yo, _, pairs, chans = out_ref.shape

    @pl.when(step == 0)
    def _():
        fill_grads(gext, g_ref, gz_ref, gy_ref, occ_ref)
        fill_taps(taps, k_ref)

    a0 = step * na
    c = chans

    def product(da, db, first, count):
        g = grad_rows(gext, a0, na, da, db)
        w = taps[first * c : (first + count) * c]
        return lax.dot_general(g, w, (((1,), (1,)), ((), ())), preferred_element_type=F32)

    mask = row_mask(occ_ref, pairs, chans)
    p00 = product(0, 0, 0, 4)
    p01 = product(0, 1, 4, 2)
    p10 = product(1, 0, 6, 2)
    p11 = product(1, 1, 8, 1)

    def put(pz, py, value):
        out_ref[:, pz, :, py] = (value.reshape(na, yo, pairs, chans) * mask).astype(BF16)

    put(0, 0, p00[:, :c])
    put(0, 1, p00[:, c : 2 * c] + p01[:, :c])
    put(1, 0, p00[:, 2 * c : 3 * c] + p10[:, :c])
    put(1, 1, (p00[:, 3 * c :] + p01[:, c:]) + (p10[:, c:] + p11))


def coarse_kernel(occ_ref, k_ref, f_ref, fz_ref, fy_ref, out_ref, prev, rim, taps):
    step = pl.program_id(0)
    na, _, yo, _, pairs, chans = f_ref.shape
    cout = out_ref.shape[3]

    @pl.when(step == 0)
    def _():
        fill_taps(taps, k_ref)
        prev[...] = fz_ref[1:].reshape(prev.shape)
        rim[0] = fz_ref[0]
        rim[1:] = fy_ref[...]

    mask = row_mask(occ_ref, pairs, chans).astype(BF16)
    even = f_ref[:, 0] * mask
    odd = f_ref[:, 1] * mask
    before = prev[...][None]
    if na > 1:
        before = jnp.concatenate([before, odd[:-1]], 0)
    prev[...] = odd[na - 1]
    z0 = 2 * na * step
    fy = rim[pl.ds(z0, 2 * na + 1)]

    def rows(planes, before, ky):
        if ky == 1:
            x = planes[:, :, 0]
        elif ky == 2:
            x = planes[:, :, 1]
        else:
            x = jnp.concatenate([before[:, None], planes[:, :-1, 1]], 1)
        return x.reshape(na * yo * pairs, chans)

    rims = fy[1:].reshape(na, 2, pairs, chans)
    edge = fy[: 2 * na].reshape(na, 2, pairs, chans)
    planes = {0: (before, edge[:, 0]), 1: (even, rims[:, 0]), 2: (odd, rims[:, 1])}
    lhs = jnp.concatenate([rows(*planes[kz], ky) for kz, ky in TAPS], 1)
    both = jnp.dot(lhs, taps[...], preferred_element_type=F32)
    both = both.reshape(na * yo, pairs, 2 * cout)
    later = pltpu.roll(both[..., cout:], 1, 1)
    first = lax.broadcasted_iota(jnp.int32, later.shape, 1) == 0
    total = both[..., :cout] + jnp.where(first, 0.0, later)
    out = total * row_mask(occ_ref, pairs, cout)
    out_ref[...] = out.reshape(na, yo, pairs, cout).astype(BF16)


def in_hbm(x):
    return pltpu.with_memory_space_constraint(x, pltpu.HBM)


def whole(shape):
    return pl.BlockSpec(shape, lambda i: (0,) * len(shape))


def leading(shape, n):
    block = (n,) + tuple(shape[1:])
    return pl.BlockSpec(block, lambda i: (i,) + (0,) * (len(shape) - 1))


SCALARS = pl.BlockSpec(memory_space=pltpu.SMEM)
PARAMS = pltpu.CompilerParams(dimension_semantics=("arbitrary",), vmem_limit_bytes=16 << 20)


def cost(flops, nbytes):
    return pl.CostEstimate(flops=int(flops), bytes_accessed=int(nbytes), transcendentals=0)


def weight_grad(occ, split, grad, cin, na=2):
    zo, yo, pairs, cout = grad.shape
    chans = 2 * cin
    shape = (9 * chans, 2 * cout)
    return pl.pallas_call(
        weight_kernel,
        grid=(zo // na,),
        in_specs=[SCALARS, leading(split.shape, na), whole(grad.shape)],
        out_specs=whole(shape),
        out_shape=jax.ShapeDtypeStruct(shape, F32),
        scratch_shapes=[pltpu.VMEM((zo + 1, yo + 1, pairs, 2 * cout), BF16)],
        compiler_params=PARAMS,
        cost_estimate=cost(2 * zo * yo * pairs * 9 * chans * 2 * cout, 2 * split.size),
    )(occ, split, grad)


def with_edges(acc, fz, fy, gz, gy):
    cin, cout = fz.shape[2] // 2, gz.shape[2]
    half = 27 * cin // 2
    part = jax.ShapeDtypeStruct((half, cout), F32)
    vmem = pl.BlockSpec(memory_space=pltpu.VMEM)
    return pl.pallas_call(
        edge_kernel,
        in_specs=[vmem] * 5,
        out_specs=[vmem] * 2,
        out_shape=[part, part],
        scratch_shapes=[pltpu.VMEM(acc.shape, F32), pltpu.VMEM((2 * half, cout), F32)],
        compiler_params=pltpu.CompilerParams(vmem_limit_bytes=12 << 20),
        cost_estimate=cost(2 * 2 * 256 * 9 * fz.shape[2] * cout, 8 * acc.size),
    )(acc, fz, fy, gz, gy)


def data_grad(occ, kernel, grad, gz, gy, na=1):
    zo, yo, pairs, cout = grad.shape
    cin = kernel.shape[1]
    chans = 2 * cin
    shape = (zo, 2, yo, 2, pairs, chans)
    return pl.pallas_call(
        data_kernel,
        grid=(zo // na,),
        in_specs=[SCALARS, whole(kernel.shape), whole(grad.shape), whole(gz.shape), whole(gy.shape)],
        out_specs=leading(shape, na),
        out_shape=jax.ShapeDtypeStruct(shape, BF16),
        scratch_shapes=[
            pltpu.VMEM((zo + 1, yo + 1, pairs, 2 * cout), BF16),
            pltpu.VMEM((9 * chans, 2 * cout), BF16),
        ],
        compiler_params=PARAMS,
        cost_estimate=cost(2 * zo * yo * pairs * 9 * chans * 2 * cout, 2 * zo * yo * pairs * 4 * chans),
    )(occ, kernel, grad, gz, gy)


def coarse_conv(occ, kernel, split, fz, fy, na=2):
    zo, _, yo, _, pairs, chans = split.shape
    cout = kernel.shape[2]
    shape = (zo, yo, pairs, cout)
    return pl.pallas_call(
        coarse_kernel,
        grid=(zo // na,),
        in_specs=[SCALARS, whole(kernel.shape), leading(split.shape, na), whole(fz.shape), whole(fy.shape)],
        out_specs=leading(shape, na),
        out_shape=jax.ShapeDtypeStruct(shape, BF16),
        scratch_shapes=[
            pltpu.VMEM((yo, 2, pairs, chans), BF16),
            pltpu.VMEM((2 * zo + 1, pairs, chans), BF16),
            pltpu.VMEM((9 * chans, 2 * cout), BF16),
        ],
        compiler_params=PARAMS,
        cost_estimate=cost(2 * zo * yo * pairs * 9 * chans * 2 * cout, 2 * split.size),
    )(occ, kernel, split, fz, fy)


def shifted(block, axis, distance):
    n = lax.axis_size(axis)
    return lax.ppermute(block, axis, [(i, i + distance) for i in range(n) if 0 <= i + distance < n])


def partners(nz, ny, other):
    moves = []
    for z in range(nz):
        for y in range(ny):
            pz, py = other(z, y)
            moves.append((z * ny + y, pz * ny + py))
    return moves


def join_kernel(a_ref, b_ref, c_ref, d_ref, out_ref):
    core, first, second = place()
    part = a_ref.shape[0]

    def put(c, f, s, value):
        at = pl.multiple_of(((c * 2 + f) * 2 + s) * part, 8)
        out_ref[pl.ds(at, part)] = value.astype(F32)

    put(core, first, second, a_ref[...])
    put(core, first, 1 - second, b_ref[...])
    put(core, 1 - first, second, c_ref[:part])
    put(core, 1 - first, 1 - second, c_ref[part:])
    put(1 - core, second, first, d_ref[:part])
    put(1 - core, second, 1 - first, d_ref[part : 2 * part])
    put(1 - core, 1 - second, first, d_ref[2 * part : 3 * part])
    put(1 - core, 1 - second, 1 - first, d_ref[3 * part :])


def summed(keep, send):
    both = ("gz", "gy")
    nz, ny = lax.axis_size("gz"), lax.axis_size("gy")
    to_core = partners(nz, ny, lambda z, y: (z, y ^ 1))
    to_first = partners(nz, ny, lambda z, y: (z ^ 1, y) if y % 2 == 0 else (z, y ^ 2))
    to_second = partners(nz, ny, lambda z, y: (z, y ^ 2) if y % 2 == 0 else (z ^ 1, y))

    def hop(x, route):
        return lax.ppermute(x, both, route)

    got = hop(send, to_core)
    for route in (to_first, to_second):
        n = keep.shape[0] // 2
        send = keep[n:] + got[n:]
        keep, mine = keep[:n], got[:n]
        got = hop(send, route)
        keep = keep + mine
    total = keep + got
    step = 2
    while step < nz:
        far = partners(nz, ny, lambda z, y: (z ^ step, y))
        total = total + hop(total, far)
        step *= 2

    a = total.astype(BF16)
    b = hop(a, to_second)
    ab = jnp.concatenate([a, b], 0)
    c = hop(ab, to_first)
    d = hop(jnp.concatenate([ab, c], 0), to_core)
    vmem = pl.BlockSpec(memory_space=pltpu.VMEM)
    return pl.pallas_call(
        join_kernel,
        in_specs=[vmem] * 4,
        out_specs=vmem,
        out_shape=jax.ShapeDtypeStruct((8 * a.shape[0], a.shape[1]), F32),
        compiler_params=pltpu.CompilerParams(vmem_limit_bytes=16 << 20),
        cost_estimate=cost(0, 8 * a.size * 6),
    )(a, b, c, d)


def shards(features, occupancy, kernel, upstream):
    nz, ny = lax.axis_size("gz"), lax.axis_size("gy")
    if ny != 4 or nz & (nz - 1) or occupancy.shape[:2] != (1, 1):
        raise ValueError("unsupported mesh")
    zi, yi, pairs, chans = features.shape
    zo, yo = zi // 2, yi // 2
    taps = kernel.reshape((27,) + kernel.shape[3:])
    split = features.reshape(zo, 2, yo, 2, pairs, chans)
    gz, gy, rz, ry = rims_of(occupancy, features, upstream)

    gy = shifted(gy, "gy", -1)
    gz = shifted(jnp.concatenate([gz, gy[:1]], 0), "gz", -1)
    acc = weight_grad(occupancy, split, upstream, chans // 2)
    keep, send = with_edges(acc, rz, ry, gz, gy)
    kernel_grad = summed(keep, send).reshape(kernel.shape)

    fy = shifted(ry, "gy", 1)
    fz = shifted(jnp.concatenate([fy[-1:], rz], 0), "gz", 1)
    coarse = coarse_conv(occupancy, taps, split, fz, fy)
    feature_grad = data_grad(occupancy, taps, upstream, gz, gy).reshape(features.shape)
    return (coarse, feature_grad, kernel_grad)


def solution(mesh):
    return jax.shard_map(
        shards,
        mesh=mesh,
        in_specs=(P("gz", "gy", None, None), P("gz", "gy", None), P(), P("gz", "gy", None, None)),
        out_specs=(P("gz", "gy", None, None), P("gz", "gy", None, None), P()),
        check_vma=False,
    )
```

```python
import functools

import jax
import jax.numpy as jnp
from jax import lax
from jax.experimental import pallas as pl
from jax.experimental.pallas import tpu as pltpu
from jax.sharding import PartitionSpec as P


F32 = jnp.float32
BF16 = jnp.bfloat16

TAPS = ((1, 1), (1, 2), (2, 1), (2, 2), (1, 0), (2, 0), (0, 1), (0, 2), (0, 0))


def row_mask(occ_ref, pairs, lanes):
    width = pairs // occ_ref.shape[2]
    block = lax.broadcasted_iota(jnp.int32, (pairs, lanes), 0) // width
    mask = jnp.zeros((pairs, lanes), F32)
    for k in range(occ_ref.shape[2]):
        here = occ_ref[0, 0, k].astype(F32)
        mask = jnp.where(block == k, here, mask)
    return mask


def with_next(g):
    pairs = g.shape[-2]
    axis = g.ndim - 2
    wide = pltpu.roll(g.astype(F32), pairs - 1, axis)
    last = lax.broadcasted_iota(jnp.int32, wide.shape, axis) == pairs - 1
    return jnp.concatenate([g, jnp.where(last, 0.0, wide).astype(BF16)], -1)


def grad_rows(gext, a0, na, da, db):
    _, yo1, pairs, wide = gext.shape
    yo = yo1 - 1
    return gext[pl.ds(a0 + da, na), db : db + yo].reshape(na * yo * pairs, wide)


def fill_taps(taps, k_ref):
    cin, cout = k_ref.shape[1:]
    for s, (kz, ky) in enumerate(TAPS):
        t = 3 * (3 * kz + ky)
        r = s * 2 * cin
        taps[r : r + 2 * cin, :cout] = k_ref[t + 1 : t + 3].reshape(2 * cin, cout)
        taps[r : r + cin, cout:] = jnp.zeros((cin, cout), BF16)
        taps[r + cin : r + 2 * cin, cout:] = k_ref[t]


def rims_of(occ, features, grad):
    zi, yi, pairs, chans = features.shape
    zo, yo, _, cout = grad.shape
    sizes = ((yo, pairs, cout), (zo, pairs, cout), (yi, pairs, chans), (zi, pairs, chans))

    def body(occ_ref, fl_ref, fb_ref, ga_ref, gb_ref, gz_ref, gy_ref, fz_ref, fy_ref):
        mask = row_mask(occ_ref, pairs, chans).astype(BF16)
        gz_ref[...] = ga_ref[0] * mask
        gy_ref[...] = gb_ref[:, 0] * mask
        fz_ref[...] = fl_ref[0] * mask
        fy_ref[...] = fb_ref[:, 0] * mask

    return pl.pallas_call(
        body,
        grid=(1,),
        in_specs=[
            SCALARS,
            pl.BlockSpec((1, yi, pairs, chans), lambda i: (zi - 1, 0, 0, 0)),
            pl.BlockSpec((zi, 1, pairs, chans), lambda i: (0, yi - 1, 0, 0)),
            pl.BlockSpec((1, yo, pairs, cout), lambda i: (0, 0, 0, 0)),
            pl.BlockSpec((zo, 1, pairs, cout), lambda i: (0, 0, 0, 0)),
        ],
        out_specs=[whole(x) for x in sizes],
        out_shape=[jax.ShapeDtypeStruct(x, BF16) for x in sizes],
        compiler_params=pltpu.CompilerParams(vmem_limit_bytes=4 << 20),
        cost_estimate=cost(0, 2 * 2 * sum(x[0] * x[1] * x[2] for x in sizes)),
    )(in_hbm(occ), in_hbm(features), in_hbm(features), in_hbm(grad), in_hbm(grad))


def weight_kernel(occ_ref, f_ref, g_ref, acc_ref, gext):
    zo, _, yo, _, pairs, chans = f_ref.shape
    cout = g_ref.shape[3]
    mask = row_mask(occ_ref, pairs, cout).astype(BF16)
    for a in range(zo):
        gext[a, :yo] = with_next(g_ref[a] * mask)
    gext[zo] = jnp.zeros(gext.shape[1:], BF16)
    gext[:, yo] = jnp.zeros((zo + 1, pairs, 2 * cout), BF16)
    mask = row_mask(occ_ref, pairs, chans).astype(BF16)

    def rows(pz, py):
        return (f_ref[:, pz, :, py] * mask).reshape(zo * yo * pairs, chans)

    ee, eo, oe, oo = rows(0, 0), rows(0, 1), rows(1, 0), rows(1, 1)
    c = chans

    def product(x, da, db):
        return rows_product(x, grad_rows(gext, 0, zo, da, db))

    acc_ref[: 4 * c] = product(jnp.concatenate([ee, eo, oe, oo], 1), 0, 0)
    acc_ref[4 * c : 6 * c] = product(jnp.concatenate([eo, oo], 1), 0, 1)
    acc_ref[6 * c : 8 * c] = product(jnp.concatenate([oe, oo], 1), 1, 0)
    acc_ref[8 * c : 9 * c] = product(oo, 1, 1)


def rows_product(x, g):
    return lax.dot_general(x, g, (((0,), (0,)), ((), ())), preferred_element_type=F32)


def place():
    z, y = lax.axis_index("gz"), lax.axis_index("gy")
    return y % 2, 2 * (z % 2) + (y // 2) % 2


def edge_kernel(acc_ref, fz_ref, fy_ref, gz_ref, gy_ref, keep_ref, send_ref, acc, flat):
    yi, pairs, chans = fz_ref.shape
    cin, cout, yo, zo = chans // 2, gz_ref.shape[2], yi // 2, gy_ref.shape[0]
    c = chans
    fz = fz_ref[...].reshape(yo, 2, pairs, chans)
    fy = fy_ref[...].reshape(zo, 2, pairs, chans)
    gz, gy = with_next(gz_ref[...]), with_next(gy_ref[...])

    def flatten(x):
        return x.reshape(x.shape[0] * pairs, x.shape[-1])

    oe, oo = flatten(fz[:, 0]), flatten(fz[:, 1])
    acc[6 * c : 8 * c] = acc_ref[6 * c : 8 * c] + rows_product(jnp.concatenate([oe, oo], 1), flatten(gz[:yo]))
    last = rows_product(oo, flatten(gz[1:]))
    eo, oo = flatten(fy[:, 0]), flatten(fy[:, 1])
    acc[4 * c : 6 * c] = acc_ref[4 * c : 6 * c] + rows_product(jnp.concatenate([eo, oo], 1), flatten(gy))
    last = last + rows_product(oo[: -pairs], flatten(gy[1:]))
    acc[8 * c :] = acc_ref[8 * c :] + last

    for s, (kz, ky) in enumerate(TAPS):
        t = 3 * (3 * kz + ky) * cin
        r = s * chans
        source = acc_ref if s < 4 else acc
        flat[t : t + cin] = source[r + cin : r + chans, cout:]
        flat[t + cin : t + 3 * cin] = source[r : r + chans, :cout]
    core, quarter = place()
    part = keep_ref.shape[0] // 4
    for r in range(4):
        rows = slice(r * part, (r + 1) * part)
        mine = (core * 4 + (quarter ^ r)) * part
        keep_ref[rows] = flat[pl.ds(pl.multiple_of(mine, 8), part)]
        its = ((1 - core) * 4 + (quarter ^ r)) * part
        send_ref[rows] = flat[pl.ds(pl.multiple_of(its, 8), part)]


def data_kernel(occ_ref, k_ref, g_ref, gz_ref, gy_ref, *rest, first):
    out_ref, gext, taps = rest[-3:]
    step = pl.program_id(0)
    na, _, yo, _, pairs, chans = out_ref.shape
    zo = g_ref.shape[0]
    count = gext.shape[0] - 1

    @pl.when(step == 0)
    def _():
        mask = row_mask(occ_ref, pairs, g_ref.shape[3]).astype(BF16)
        for a in range(count + 1):
            if first + a < zo:
                gext[a, :yo] = with_next(g_ref[first + a] * mask)
        near = min(count + 1, zo - first)
        gext[:near, yo] = with_next(gy_ref[first : first + near])
        if near == count:
            gext[count] = with_next(gz_ref[...])
        fill_taps(taps, k_ref)

    a0 = step * na
    c = chans

    def product(da, db, at, n):
        g = grad_rows(gext, a0, na, da, db)
        w = taps[at * c : (at + n) * c]
        return lax.dot_general(g, w, (((1,), (1,)), ((), ())), preferred_element_type=F32)

    mask = row_mask(occ_ref, pairs, chans)
    p00 = product(0, 0, 0, 4)
    p01 = product(0, 1, 4, 2)
    p10 = product(1, 0, 6, 2)
    p11 = product(1, 1, 8, 1)

    def put(pz, py, value):
        out_ref[:, pz, :, py] = (value.reshape(na, yo, pairs, chans) * mask).astype(BF16)

    put(0, 0, p00[:, :c])
    put(0, 1, p00[:, c : 2 * c] + p01[:, :c])
    put(1, 0, p00[:, 2 * c : 3 * c] + p10[:, :c])
    put(1, 1, (p00[:, 3 * c :] + p01[:, c:]) + (p10[:, c:] + p11))


def coarse_kernel(occ_ref, k_ref, f_ref, before_ref, fy_ref, *rest, first):
    out_ref, prev, rim, taps = rest[-4:]
    step = pl.program_id(0)
    na, _, yo, _, pairs, chans = f_ref.shape
    cout = out_ref.shape[3]

    @pl.when(step == 0)
    def _():
        fill_taps(taps, k_ref)
        if first == 0:
            prev[...] = before_ref[1:].reshape(prev.shape)
            rim[0] = before_ref[0]
            rim[1:] = fy_ref[: rim.shape[0] - 1]
        else:
            prev[...] = before_ref[0, 1] * row_mask(occ_ref, pairs, chans).astype(BF16)
            rim[...] = fy_ref[2 * first - 1 : 2 * first - 1 + rim.shape[0]]

    mask = row_mask(occ_ref, pairs, chans).astype(BF16)
    even = f_ref[:, 0] * mask
    odd = f_ref[:, 1] * mask
    before = prev[...][None]
    if na > 1:
        before = jnp.concatenate([before, odd[:-1]], 0)
    prev[...] = odd[na - 1]
    z0 = 2 * na * step
    fy = rim[pl.ds(z0, 2 * na + 1)]

    def rows(planes, before, ky):
        if ky == 1:
            x = planes[:, :, 0]
        elif ky == 2:
            x = planes[:, :, 1]
        else:
            x = jnp.concatenate([before[:, None], planes[:, :-1, 1]], 1)
        return x.reshape(na * yo * pairs, chans)

    rims = fy[1:].reshape(na, 2, pairs, chans)
    edge = fy[: 2 * na].reshape(na, 2, pairs, chans)
    planes = {0: (before, edge[:, 0]), 1: (even, rims[:, 0]), 2: (odd, rims[:, 1])}
    lhs = jnp.concatenate([rows(*planes[kz], ky) for kz, ky in TAPS], 1)
    both = jnp.dot(lhs, taps[...], preferred_element_type=F32)
    both = both.reshape(na * yo, pairs, 2 * cout)
    later = pltpu.roll(both[..., cout:], 1, 1)
    first = lax.broadcasted_iota(jnp.int32, later.shape, 1) == 0
    total = both[..., :cout] + jnp.where(first, 0.0, later)
    out = total * row_mask(occ_ref, pairs, cout)
    out_ref[...] = out.reshape(na, yo, pairs, cout).astype(BF16)


def in_hbm(x):
    return pltpu.with_memory_space_constraint(x, pltpu.HBM)


def whole(shape):
    return pl.BlockSpec(shape, lambda i: (0,) * len(shape))


SCALARS = pl.BlockSpec(memory_space=pltpu.SMEM)
PARAMS = pltpu.CompilerParams(dimension_semantics=("arbitrary",), vmem_limit_bytes=16 << 20)


def cost(flops, nbytes):
    return pl.CostEstimate(flops=int(flops), bytes_accessed=int(nbytes), transcendentals=0)


def weight_grad(occ, split, grad, cin):
    zo, yo, pairs, cout = grad.shape
    chans = 2 * cin
    shape = (9 * chans, 2 * cout)
    vmem = pl.BlockSpec(memory_space=pltpu.VMEM)
    return pl.pallas_call(
        weight_kernel,
        in_specs=[SCALARS, vmem, vmem],
        out_specs=vmem,
        out_shape=jax.ShapeDtypeStruct(shape, F32),
        scratch_shapes=[pltpu.VMEM((zo + 1, yo + 1, pairs, 2 * cout), BF16)],
        compiler_params=pltpu.CompilerParams(vmem_limit_bytes=16 << 20),
        cost_estimate=cost(2 * zo * yo * pairs * 9 * chans * 2 * cout, 2 * split.size),
    )(occ, split, grad)


def with_edges(acc, fz, fy, gz, gy):
    cin, cout = fz.shape[2] // 2, gz.shape[2]
    half = 27 * cin // 2
    part = jax.ShapeDtypeStruct((half, cout), F32)
    vmem = pl.BlockSpec(memory_space=pltpu.VMEM)
    return pl.pallas_call(
        edge_kernel,
        in_specs=[vmem] * 5,
        out_specs=[vmem] * 2,
        out_shape=[part, part],
        scratch_shapes=[pltpu.VMEM(acc.shape, F32), pltpu.VMEM((2 * half, cout), F32)],
        compiler_params=pltpu.CompilerParams(vmem_limit_bytes=12 << 20),
        cost_estimate=cost(2 * 2 * 256 * 9 * fz.shape[2] * cout, 8 * acc.size),
    )(acc, fz, fy, gz, gy)


def data_grad(occ, kernel, grad, gz, gy, first, count, into=None, na=2):
    zo, yo, pairs, cout = grad.shape
    cin = kernel.shape[1]
    chans = 2 * cin
    shape = (zo, 2, yo, 2, pairs, chans)
    block = pl.BlockSpec((na,) + shape[1:], lambda i: (i + first // na, 0, 0, 0, 0, 0))
    given = () if into is None else (into,)
    return pl.pallas_call(
        functools.partial(data_kernel, first=first),
        grid=(count // na,),
        in_specs=[SCALARS, whole(kernel.shape), whole(grad.shape), whole(gz.shape), whole(gy.shape)]
        + [pl.BlockSpec(memory_space=pl.ANY)] * len(given),
        out_specs=block,
        out_shape=jax.ShapeDtypeStruct(shape, BF16),
        scratch_shapes=[
            pltpu.VMEM((count + 1, yo + 1, pairs, 2 * cout), BF16),
            pltpu.VMEM((9 * chans, 2 * cout), BF16),
        ],
        input_output_aliases={5: 0} if given else {},
        compiler_params=PARAMS,
        cost_estimate=cost(2 * count * yo * pairs * 9 * chans * 2 * cout, 2 * count * yo * pairs * 4 * chans),
    )(occ, kernel, grad, gz, gy, *given)


def coarse_conv(occ, kernel, split, before, fy, first, count, into=None, na=2):
    zo, _, yo, _, pairs, chans = split.shape
    cout = kernel.shape[2]
    shape = (zo, yo, pairs, cout)
    given = () if into is None else (into,)
    if first == 0:
        ahead = whole(before.shape)
    else:
        ahead = pl.BlockSpec((1,) + split.shape[1:], lambda i: (first - 1, 0, 0, 0, 0, 0))
    return pl.pallas_call(
        functools.partial(coarse_kernel, first=first),
        grid=(count // na,),
        in_specs=[
            SCALARS,
            whole(kernel.shape),
            pl.BlockSpec((na,) + split.shape[1:], lambda i: (i + first // na, 0, 0, 0, 0, 0)),
            ahead,
            whole(fy.shape),
        ]
        + [pl.BlockSpec(memory_space=pl.ANY)] * len(given),
        out_specs=pl.BlockSpec((na,) + shape[1:], lambda i: (i + first // na, 0, 0, 0)),
        out_shape=jax.ShapeDtypeStruct(shape, BF16),
        scratch_shapes=[
            pltpu.VMEM((yo, 2, pairs, chans), BF16),
            pltpu.VMEM((2 * count + 1, pairs, chans), BF16),
            pltpu.VMEM((9 * chans, 2 * cout), BF16),
        ],
        input_output_aliases={5: 0} if given else {},
        compiler_params=PARAMS,
        cost_estimate=cost(2 * count * yo * pairs * 9 * chans * 2 * cout, 2 * split.size),
    )(occ, kernel, split, before, fy, *given)


def shifted(block, axis, distance):
    n = lax.axis_size(axis)
    return lax.ppermute(block, axis, [(i, i + distance) for i in range(n) if 0 <= i + distance < n])


def partners(nz, ny, other):
    moves = []
    for z in range(nz):
        for y in range(ny):
            pz, py = other(z, y)
            moves.append((z * ny + y, pz * ny + py))
    return moves


def join_kernel(*refs, other):
    out_ref, wide, sem = refs[-3:]
    core, quarter = place()
    half, part = wide.shape[0], wide.shape[0] // 4
    copies = []
    for r in range(4):
        value = refs[0][r * part : (r + 1) * part] if other else refs[r][...]
        wide[r * part : (r + 1) * part] = value.astype(F32)
        at = ((core ^ 1) if other else core) * half + (quarter ^ r) * part
        to = out_ref.at[pl.ds(pl.multiple_of(at, 8), part)]
        copies.append(pltpu.make_async_copy(wide.at[pl.ds(r * part, part)], to, sem.at[r]))
        copies[-1].start()
    for copy in copies:
        copy.wait()


def joined(parts, other, into=None):
    rows = sum(x.shape[0] for x in parts)
    cols = parts[0].shape[1]
    given = () if into is None else (into,)
    return pl.pallas_call(
        functools.partial(join_kernel, other=other),
        in_specs=[pl.BlockSpec(memory_space=pltpu.VMEM)] * len(parts)
        + [pl.BlockSpec(memory_space=pl.ANY)] * len(given),
        out_specs=pl.BlockSpec(memory_space=pl.ANY),
        out_shape=jax.ShapeDtypeStruct((2 * rows, cols), F32),
        scratch_shapes=[pltpu.VMEM((rows, cols), F32), pltpu.SemaphoreType.DMA((4,))],
        input_output_aliases={len(parts): 0} if given else {},
        compiler_params=pltpu.CompilerParams(vmem_limit_bytes=4 << 20),
        cost_estimate=cost(0, 6 * rows * cols),
    )(*parts, *given)


def summed(keep, send):
    both = ("gz", "gy")
    nz, ny = lax.axis_size("gz"), lax.axis_size("gy")

    def hop(x, flip_z, flip_y):
        return lax.ppermute(x, both, partners(nz, ny, lambda z, y: (z ^ flip_z, y ^ flip_y)))

    def around(values):
        return {r: hop(values[r], r >> 1, 2 * (r & 1)) for r in (3, 2, 1)}

    got = hop(send, 0, 1)
    n = keep.shape[0] // 4
    sums = [keep[r * n : (r + 1) * n] + got[r * n : (r + 1) * n] for r in range(4)]
    near = around(sums)
    total = (sums[0] + near[3]) + (near[2] + near[1])
    step = 2
    while step < nz:
        total = total + hop(total, step, 0)
        step *= 2

    own = total.astype(BF16)
    back = around([own] * 4)
    parts = (own, back[1], back[2], back[3])
    other = hop(jnp.concatenate(parts, 0), 0, 1)
    out = joined(parts, False)
    return joined((other,), True, out)


def shards(features, occupancy, kernel, upstream):
    nz, ny = lax.axis_size("gz"), lax.axis_size("gy")
    if ny != 4 or nz & (nz - 1) or occupancy.shape[:2] != (1, 1):
        raise ValueError("unsupported mesh")
    zi, yi, pairs, chans = features.shape
    zo, yo = zi // 2, yi // 2
    taps = kernel.reshape((27,) + kernel.shape[3:])
    split = features.reshape(zo, 2, yo, 2, pairs, chans)
    gz, gy, rz, ry = rims_of(occupancy, features, upstream)

    gy = shifted(gy, "gy", -1)
    gz = shifted(jnp.concatenate([gz, gy[:1]], 0), "gz", -1)
    acc = weight_grad(occupancy, split, upstream, chans // 2)
    keep, send = with_edges(acc, rz, ry, gz, gy)
    kernel_grad = summed(keep, send).reshape(kernel.shape)

    fy = shifted(ry, "gy", 1)
    fz = shifted(jnp.concatenate([fy[-1:], rz], 0), "gz", 1)
    mid = zo // 2
    coarse = coarse_conv(occupancy, taps, split, split, fy, mid, zo - mid)
    coarse = coarse_conv(occupancy, taps, split, fz, fy, 0, mid, coarse)
    given = (occupancy, taps, upstream, gz, gy)
    low = data_grad(*given, 0, mid)
    feature_grad = data_grad(*given, mid, zo - mid, low).reshape(features.shape)
    return (coarse, feature_grad, kernel_grad)


def solution(mesh):
    return jax.shard_map(
        shards,
        mesh=mesh,
        in_specs=(P("gz", "gy", None, None), P("gz", "gy", None), P(), P("gz", "gy", None, None)),
        out_specs=(P("gz", "gy", None, None), P("gz", "gy", None, None), P()),
        check_vma=False,
    )
```

```python
import functools

import jax
import jax.numpy as jnp
from jax import lax
from jax.experimental import pallas as pl
from jax.experimental.pallas import tpu as pltpu
from jax.sharding import PartitionSpec as P


F32 = jnp.float32
BF16 = jnp.bfloat16

TAPS = ((1, 1), (1, 2), (2, 1), (2, 2), (1, 0), (2, 0), (0, 1), (0, 2), (0, 0))


def row_mask(occ_ref, pairs, lanes):
    width = pairs // occ_ref.shape[2]
    block = lax.broadcasted_iota(jnp.int32, (pairs, lanes), 0) // width
    mask = jnp.zeros((pairs, lanes), F32)
    for k in range(occ_ref.shape[2]):
        here = occ_ref[0, 0, k].astype(F32)
        mask = jnp.where(block == k, here, mask)
    return mask


def with_next(g):
    pairs = g.shape[-2]
    axis = g.ndim - 2
    wide = pltpu.roll(g.astype(F32), pairs - 1, axis)
    last = lax.broadcasted_iota(jnp.int32, wide.shape, axis) == pairs - 1
    return jnp.concatenate([g, jnp.where(last, 0.0, wide).astype(BF16)], -1)


def grad_rows(gext, a0, na, da, db):
    _, yo1, pairs, wide = gext.shape
    yo = yo1 - 1
    return gext[pl.ds(a0 + da, na), db : db + yo].reshape(na * yo * pairs, wide)


def fill_taps(taps, k_ref):
    cin, cout = k_ref.shape[1:]
    for s, (kz, ky) in enumerate(TAPS):
        t = 3 * (3 * kz + ky)
        r = s * 2 * cin
        taps[r : r + 2 * cin, :cout] = k_ref[t + 1 : t + 3].reshape(2 * cin, cout)
        taps[r : r + cin, cout:] = jnp.zeros((cin, cout), BF16)
        taps[r + cin : r + 2 * cin, cout:] = k_ref[t]


def rims_of(occ, features, grad):
    zi, yi, pairs, chans = features.shape
    zo, yo, _, cout = grad.shape
    sizes = ((yo, pairs, cout), (zo, pairs, cout), (yi, pairs, chans), (zi, pairs, chans))

    def body(occ_ref, fl_ref, fb_ref, ga_ref, gb_ref, gz_ref, gy_ref, fz_ref, fy_ref):
        mask = row_mask(occ_ref, pairs, chans).astype(BF16)
        gz_ref[...] = ga_ref[0] * mask
        gy_ref[...] = gb_ref[:, 0] * mask
        fz_ref[...] = fl_ref[0] * mask
        fy_ref[...] = fb_ref[:, 0] * mask

    return pl.pallas_call(
        body,
        grid=(1,),
        in_specs=[
            SCALARS,
            pl.BlockSpec((1, yi, pairs, chans), lambda i: (zi - 1, 0, 0, 0)),
            pl.BlockSpec((zi, 1, pairs, chans), lambda i: (0, yi - 1, 0, 0)),
            pl.BlockSpec((1, yo, pairs, cout), lambda i: (0, 0, 0, 0)),
            pl.BlockSpec((zo, 1, pairs, cout), lambda i: (0, 0, 0, 0)),
        ],
        out_specs=[whole(x) for x in sizes],
        out_shape=[jax.ShapeDtypeStruct(x, BF16) for x in sizes],
        compiler_params=pltpu.CompilerParams(vmem_limit_bytes=4 << 20),
        cost_estimate=cost(0, 2 * 2 * sum(x[0] * x[1] * x[2] for x in sizes)),
    )(in_hbm(occ), in_hbm(features), in_hbm(features), in_hbm(grad), in_hbm(grad))


def weight_kernel(occ_ref, f_ref, g_ref, acc_ref, gext):
    zo, _, yo, _, pairs, chans = f_ref.shape
    cout = g_ref.shape[3]
    mask = row_mask(occ_ref, pairs, cout).astype(BF16)
    for a in range(zo):
        gext[a, :yo] = with_next(g_ref[a] * mask)
    gext[zo] = jnp.zeros(gext.shape[1:], BF16)
    gext[:, yo] = jnp.zeros((zo + 1, pairs, 2 * cout), BF16)
    mask = row_mask(occ_ref, pairs, chans).astype(BF16)

    def rows(pz, py):
        return (f_ref[:, pz, :, py] * mask).reshape(zo * yo * pairs, chans)

    ee, eo, oe, oo = rows(0, 0), rows(0, 1), rows(1, 0), rows(1, 1)
    c = chans

    def product(x, da, db):
        return rows_product(x, grad_rows(gext, 0, zo, da, db))

    acc_ref[: 4 * c] = product(jnp.concatenate([ee, eo, oe, oo], 1), 0, 0)
    acc_ref[4 * c : 6 * c] = product(jnp.concatenate([eo, oo], 1), 0, 1)
    acc_ref[6 * c : 8 * c] = product(jnp.concatenate([oe, oo], 1), 1, 0)
    acc_ref[8 * c : 9 * c] = product(oo, 1, 1)


def rows_product(x, g):
    return lax.dot_general(x, g, (((0,), (0,)), ((), ())), preferred_element_type=F32)


def place():
    z, y = lax.axis_index("gz"), lax.axis_index("gy")
    return y % 2, 2 * (z % 2) + (y // 2) % 2


def edge_kernel(acc_ref, fz_ref, fy_ref, gz_ref, gy_ref, keep_ref, send_ref, acc, flat):
    yi, pairs, chans = fz_ref.shape
    cin, cout, yo, zo = chans // 2, gz_ref.shape[2], yi // 2, gy_ref.shape[0]
    c = chans
    fz = fz_ref[...].reshape(yo, 2, pairs, chans)
    fy = fy_ref[...].reshape(zo, 2, pairs, chans)
    gz, gy = with_next(gz_ref[...]), with_next(gy_ref[...])

    def flatten(x):
        return x.reshape(x.shape[0] * pairs, x.shape[-1])

    oe, oo = flatten(fz[:, 0]), flatten(fz[:, 1])
    acc[6 * c : 8 * c] = acc_ref[6 * c : 8 * c] + rows_product(jnp.concatenate([oe, oo], 1), flatten(gz[:yo]))
    last = rows_product(oo, flatten(gz[1:]))
    eo, oo = flatten(fy[:, 0]), flatten(fy[:, 1])
    acc[4 * c : 6 * c] = acc_ref[4 * c : 6 * c] + rows_product(jnp.concatenate([eo, oo], 1), flatten(gy))
    last = last + rows_product(oo[: -pairs], flatten(gy[1:]))
    acc[8 * c :] = acc_ref[8 * c :] + last

    for s, (kz, ky) in enumerate(TAPS):
        t = 3 * (3 * kz + ky) * cin
        r = s * chans
        source = acc_ref if s < 4 else acc
        flat[t : t + cin] = source[r + cin : r + chans, cout:]
        flat[t + cin : t + 3 * cin] = source[r : r + chans, :cout]
    core, quarter = place()
    part = keep_ref.shape[0] // 4
    for r in range(4):
        rows = slice(r * part, (r + 1) * part)
        mine = (core * 4 + (quarter ^ r)) * part
        keep_ref[rows] = flat[pl.ds(pl.multiple_of(mine, 8), part)]
        its = ((1 - core) * 4 + (quarter ^ r)) * part
        send_ref[rows] = flat[pl.ds(pl.multiple_of(its, 8), part)]


def data_kernel(occ_ref, k_ref, g_ref, gz_ref, gy_ref, *rest, first):
    out_ref, gext, taps = rest[-3:]
    step = pl.program_id(0)
    na, _, yo, _, pairs, chans = out_ref.shape
    zo = g_ref.shape[0]
    count = gext.shape[0] - 1

    @pl.when(step == 0)
    def _():
        mask = row_mask(occ_ref, pairs, g_ref.shape[3]).astype(BF16)
        for a in range(count + 1):
            if first + a < zo:
                gext[a, :yo] = with_next(g_ref[first + a] * mask)
        near = min(count + 1, zo - first)
        gext[:near, yo] = with_next(gy_ref[first : first + near])
        if near == count:
            gext[count] = with_next(gz_ref[...])
        fill_taps(taps, k_ref)

    a0 = step * na
    c = chans

    def product(da, db, at, n):
        g = grad_rows(gext, a0, na, da, db)
        w = taps[at * c : (at + n) * c]
        return lax.dot_general(g, w, (((1,), (1,)), ((), ())), preferred_element_type=F32)

    mask = row_mask(occ_ref, pairs, chans)
    p00 = product(0, 0, 0, 4)
    p01 = product(0, 1, 4, 2)
    p10 = product(1, 0, 6, 2)
    p11 = product(1, 1, 8, 1)

    def put(pz, py, value):
        out_ref[:, pz, :, py] = (value.reshape(na, yo, pairs, chans) * mask).astype(BF16)

    put(0, 0, p00[:, :c])
    put(0, 1, p00[:, c : 2 * c] + p01[:, :c])
    put(1, 0, p00[:, 2 * c : 3 * c] + p10[:, :c])
    put(1, 1, (p00[:, 3 * c :] + p01[:, c:]) + (p10[:, c:] + p11))


def coarse_kernel(occ_ref, k_ref, f_ref, before_ref, fy_ref, *rest, first):
    out_ref, prev, rim, taps = rest[-4:]
    step = pl.program_id(0)
    na, _, yo, _, pairs, chans = f_ref.shape
    cout = out_ref.shape[3]

    @pl.when(step == 0)
    def _():
        fill_taps(taps, k_ref)
        if first == 0:
            prev[...] = before_ref[1:].reshape(prev.shape)
            rim[0] = before_ref[0]
            rim[1:] = fy_ref[: rim.shape[0] - 1]
        else:
            prev[...] = before_ref[0, 1] * row_mask(occ_ref, pairs, chans).astype(BF16)
            rim[...] = fy_ref[2 * first - 1 : 2 * first - 1 + rim.shape[0]]

    mask = row_mask(occ_ref, pairs, chans).astype(BF16)
    even = f_ref[:, 0] * mask
    odd = f_ref[:, 1] * mask
    before = prev[...][None]
    if na > 1:
        before = jnp.concatenate([before, odd[:-1]], 0)
    prev[...] = odd[na - 1]
    z0 = 2 * na * step
    fy = rim[pl.ds(z0, 2 * na + 1)]

    def rows(planes, before, ky):
        if ky == 1:
            x = planes[:, :, 0]
        elif ky == 2:
            x = planes[:, :, 1]
        else:
            x = jnp.concatenate([before[:, None], planes[:, :-1, 1]], 1)
        return x.reshape(na * yo * pairs, chans)

    rims = fy[1:].reshape(na, 2, pairs, chans)
    edge = fy[: 2 * na].reshape(na, 2, pairs, chans)
    planes = {0: (before, edge[:, 0]), 1: (even, rims[:, 0]), 2: (odd, rims[:, 1])}
    lhs = jnp.concatenate([rows(*planes[kz], ky) for kz, ky in TAPS], 1)
    both = jnp.dot(lhs, taps[...], preferred_element_type=F32)
    both = both.reshape(na * yo, pairs, 2 * cout)
    later = pltpu.roll(both[..., cout:], 1, 1)
    first = lax.broadcasted_iota(jnp.int32, later.shape, 1) == 0
    total = both[..., :cout] + jnp.where(first, 0.0, later)
    out = total * row_mask(occ_ref, pairs, cout)
    out_ref[...] = out.reshape(na, yo, pairs, cout).astype(BF16)


def in_hbm(x):
    return pltpu.with_memory_space_constraint(x, pltpu.HBM)


def whole(shape):
    return pl.BlockSpec(shape, lambda i: (0,) * len(shape))


SCALARS = pl.BlockSpec(memory_space=pltpu.SMEM)
PARAMS = pltpu.CompilerParams(dimension_semantics=("arbitrary",), vmem_limit_bytes=16 << 20)


def cost(flops, nbytes):
    return pl.CostEstimate(flops=int(flops), bytes_accessed=int(nbytes), transcendentals=0)


def weight_grad(occ, split, grad, cin):
    zo, yo, pairs, cout = grad.shape
    chans = 2 * cin
    shape = (9 * chans, 2 * cout)
    vmem = pl.BlockSpec(memory_space=pltpu.VMEM)
    return pl.pallas_call(
        weight_kernel,
        in_specs=[SCALARS, vmem, vmem],
        out_specs=vmem,
        out_shape=jax.ShapeDtypeStruct(shape, F32),
        scratch_shapes=[pltpu.VMEM((zo + 1, yo + 1, pairs, 2 * cout), BF16)],
        compiler_params=pltpu.CompilerParams(vmem_limit_bytes=16 << 20),
        cost_estimate=cost(2 * zo * yo * pairs * 9 * chans * 2 * cout, 2 * split.size),
    )(occ, split, grad)


def with_edges(acc, fz, fy, gz, gy):
    cin, cout = fz.shape[2] // 2, gz.shape[2]
    half = 27 * cin // 2
    part = jax.ShapeDtypeStruct((half, cout), F32)
    vmem = pl.BlockSpec(memory_space=pltpu.VMEM)
    return pl.pallas_call(
        edge_kernel,
        in_specs=[vmem] * 5,
        out_specs=[vmem] * 2,
        out_shape=[part, part],
        scratch_shapes=[pltpu.VMEM(acc.shape, F32), pltpu.VMEM((2 * half, cout), F32)],
        compiler_params=pltpu.CompilerParams(vmem_limit_bytes=12 << 20),
        cost_estimate=cost(2 * 2 * 256 * 9 * fz.shape[2] * cout, 8 * acc.size),
    )(acc, fz, fy, gz, gy)


def data_grad(occ, kernel, grad, gz, gy, first, count, into=None, na=4):
    zo, yo, pairs, cout = grad.shape
    cin = kernel.shape[1]
    chans = 2 * cin
    shape = (zo, 2, yo, 2, pairs, chans)
    block = pl.BlockSpec((na,) + shape[1:], lambda i: (i + first // na, 0, 0, 0, 0, 0))
    given = () if into is None else (into,)
    return pl.pallas_call(
        functools.partial(data_kernel, first=first),
        grid=(count // na,),
        in_specs=[SCALARS, whole(kernel.shape), whole(grad.shape), whole(gz.shape), whole(gy.shape)]
        + [pl.BlockSpec(memory_space=pl.ANY)] * len(given),
        out_specs=block,
        out_shape=jax.ShapeDtypeStruct(shape, BF16),
        scratch_shapes=[
            pltpu.VMEM((count + 1, yo + 1, pairs, 2 * cout), BF16),
            pltpu.VMEM((9 * chans, 2 * cout), BF16),
        ],
        input_output_aliases={5: 0} if given else {},
        compiler_params=PARAMS,
        cost_estimate=cost(2 * count * yo * pairs * 9 * chans * 2 * cout, 2 * count * yo * pairs * 4 * chans),
    )(occ, kernel, grad, gz, gy, *given)


def coarse_conv(occ, kernel, split, before, fy, first, count, into=None, na=2):
    zo, _, yo, _, pairs, chans = split.shape
    cout = kernel.shape[2]
    shape = (zo, yo, pairs, cout)
    given = () if into is None else (into,)
    if first == 0:
        ahead = whole(before.shape)
    else:
        ahead = pl.BlockSpec((1,) + split.shape[1:], lambda i: (first - 1, 0, 0, 0, 0, 0))
    return pl.pallas_call(
        functools.partial(coarse_kernel, first=first),
        grid=(count // na,),
        in_specs=[
            SCALARS,
            whole(kernel.shape),
            pl.BlockSpec((na,) + split.shape[1:], lambda i: (i + first // na, 0, 0, 0, 0, 0)),
            ahead,
            whole(fy.shape),
        ]
        + [pl.BlockSpec(memory_space=pl.ANY)] * len(given),
        out_specs=pl.BlockSpec((na,) + shape[1:], lambda i: (i + first // na, 0, 0, 0)),
        out_shape=jax.ShapeDtypeStruct(shape, BF16),
        scratch_shapes=[
            pltpu.VMEM((yo, 2, pairs, chans), BF16),
            pltpu.VMEM((2 * count + 1, pairs, chans), BF16),
            pltpu.VMEM((9 * chans, 2 * cout), BF16),
        ],
        input_output_aliases={5: 0} if given else {},
        compiler_params=PARAMS,
        cost_estimate=cost(2 * count * yo * pairs * 9 * chans * 2 * cout, 2 * split.size),
    )(occ, kernel, split, before, fy, *given)


def shifted(block, axis, distance):
    n = lax.axis_size(axis)
    return lax.ppermute(block, axis, [(i, i + distance) for i in range(n) if 0 <= i + distance < n])


def partners(nz, ny, other):
    moves = []
    for z in range(nz):
        for y in range(ny):
            pz, py = other(z, y)
            moves.append((z * ny + y, pz * ny + py))
    return moves


def join_kernel(*refs, other):
    out_ref, wide, sem = refs[-3:]
    core, quarter = place()
    half, part = wide.shape[0], wide.shape[0] // 4
    copies = []
    for r in range(4):
        value = refs[0][r * part : (r + 1) * part] if other else refs[r][...]
        wide[r * part : (r + 1) * part] = value.astype(F32)
        at = ((core ^ 1) if other else core) * half + (quarter ^ r) * part
        to = out_ref.at[pl.ds(pl.multiple_of(at, 8), part)]
        copies.append(pltpu.make_async_copy(wide.at[pl.ds(r * part, part)], to, sem.at[r]))
        copies[-1].start()
    for copy in copies:
        copy.wait()


def joined(parts, other, into=None):
    rows = sum(x.shape[0] for x in parts)
    cols = parts[0].shape[1]
    given = () if into is None else (into,)
    return pl.pallas_call(
        functools.partial(join_kernel, other=other),
        in_specs=[pl.BlockSpec(memory_space=pltpu.VMEM)] * len(parts)
        + [pl.BlockSpec(memory_space=pl.ANY)] * len(given),
        out_specs=pl.BlockSpec(memory_space=pl.ANY),
        out_shape=jax.ShapeDtypeStruct((2 * rows, cols), F32),
        scratch_shapes=[pltpu.VMEM((rows, cols), F32), pltpu.SemaphoreType.DMA((4,))],
        input_output_aliases={len(parts): 0} if given else {},
        compiler_params=pltpu.CompilerParams(vmem_limit_bytes=4 << 20),
        cost_estimate=cost(0, 6 * rows * cols),
    )(*parts, *given)


def summed(keep, send):
    both = ("gz", "gy")
    nz, ny = lax.axis_size("gz"), lax.axis_size("gy")

    def hop(x, flip_z, flip_y):
        return lax.ppermute(x, both, partners(nz, ny, lambda z, y: (z ^ flip_z, y ^ flip_y)))

    def around(values):
        return {r: hop(values[r], r >> 1, 2 * (r & 1)) for r in (3, 2, 1)}

    got = hop(send, 0, 1)
    n = keep.shape[0] // 4
    sums = [keep[r * n : (r + 1) * n] + got[r * n : (r + 1) * n] for r in range(4)]
    near = around(sums)
    total = (sums[0] + near[3]) + (near[2] + near[1])
    step = 2
    while step < nz:
        total = total + hop(total, step, 0)
        step *= 2

    own = total.astype(BF16)
    back = around([own] * 4)
    parts = (own, back[1], back[2], back[3])
    other = hop(jnp.concatenate(parts, 0), 0, 1)
    out = joined(parts, False)
    return joined((other,), True, out)


def shards(features, occupancy, kernel, upstream):
    nz, ny = lax.axis_size("gz"), lax.axis_size("gy")
    if ny != 4 or nz & (nz - 1) or occupancy.shape[:2] != (1, 1):
        raise ValueError("unsupported mesh")
    zi, yi, pairs, chans = features.shape
    zo, yo = zi // 2, yi // 2
    taps = kernel.reshape((27,) + kernel.shape[3:])
    split = features.reshape(zo, 2, yo, 2, pairs, chans)
    gz, gy, rz, ry = rims_of(occupancy, features, upstream)

    gy = shifted(gy, "gy", -1)
    gz = shifted(jnp.concatenate([gz, gy[:1]], 0), "gz", -1)
    acc = weight_grad(occupancy, split, upstream, chans // 2)
    keep, send = with_edges(acc, rz, ry, gz, gy)
    kernel_grad = summed(keep, send).reshape(kernel.shape)

    fy = shifted(ry, "gy", 1)
    fz = shifted(jnp.concatenate([fy[-1:], rz], 0), "gz", 1)
    mid, late = zo // 2, zo - zo // 4
    coarse = coarse_conv(occupancy, taps, split, split, fy, late, zo - late)
    coarse = coarse_conv(occupancy, taps, split, fz, fy, 0, late, coarse, na=3)
    given = (occupancy, taps, upstream, gz, gy)
    low = data_grad(*given, 0, mid)
    feature_grad = data_grad(*given, mid, zo - mid, low).reshape(features.shape)
    return (coarse, feature_grad, kernel_grad)


def solution(mesh):
    return jax.shard_map(
        shards,
        mesh=mesh,
        in_specs=(P("gz", "gy", None, None), P("gz", "gy", None), P(), P("gz", "gy", None, None)),
        out_specs=(P("gz", "gy", None, None), P("gz", "gy", None, None), P()),
        check_vma=False,
    )
```
